32 devices in a mesh: row: 4 (over x, core), col: 8 (over z, y).
Axes of the slice: x: 2, y: 2, z: 4, core: 2. Of those that a mesh axis runs over, the one named last changes fastest.
Arguments:
- optical_field: float32 [2, 512, 4096], P(None, 'row', 'col'), may hold values from -6 to 6
- index_panels: bfloat16 [5, 512, 4096], P(None, ('row', 'col')), may hold values from -4 to 4
Outputs:
- propagated: float32 [2, 512, 4096], P(None, 'row', 'col')
The draws below stay inside these ranges and needn't reach their ends.
All inputs are finite; a program needn't handle non-finite values.
Results may differ from the reference program's by a relative error of at most 0.0003.
Values may be sent and summed in bfloat16 or wider, within the bound.
A program may use at most 64 MiB of HBM per device.

```python
import jax
import jax.numpy as jnp

STEPS = 2
PLANES = 5
NY = 512
NX = 4096


def levels(key, shape, pieces, least, top_value):
    def one(axis_at, parts):
        steps = jax.random.uniform(jax.random.fold_in(jax.random.fold_in(key, 6), axis_at), (parts,), jnp.float32, least / len(pieces), top_value / len(pieces))
        return jnp.repeat(jnp.exp(steps), shape[axis_at] // parts).reshape((-1,) + (1,) * (len(shape) - axis_at - 1))

    factor_of = one(*pieces[0])
    for cut in pieces[1:]:
        factor_of = factor_of * one(*cut)
    return factor_of


def gaussian(rng, extent, spread, bound, cuts=(), held_as=jnp.bfloat16):
    result = jax.random.normal(rng, extent, jnp.float32) * spread
    if len(cuts) > 0:
        result = levels(rng, extent, cuts, -0.22, 0.18) * result
    return jnp.clip(result, min=-bound, max=bound).astype(held_as)


def setup_inputs(seed: int = 0) -> dict:
    splits = jax.random.split(jax.random.key(seed), 3)
    optical_field = gaussian(splits[0], (2, NY, NX), 1.0, 6.0, ((1, 4), (2, 8)), jnp.float32)
    index_panels = gaussian(splits[1], (PLANES, NY, NX), 1.0, 4.0, ((1, 32),))
    return {"optical_field": optical_field, "index_panels": index_panels}


diffraction = 0.15
phase_gain = 0.25


def laplace(values):
    along_y = 16.0 * (jnp.roll(values, 1, 1) + jnp.roll(values, -1, 1)) - (jnp.roll(values, 2, 1) + jnp.roll(values, -2, 1))
    along_x = 16.0 * (jnp.roll(values, 1, 2) + jnp.roll(values, -1, 2)) - (jnp.roll(values, 2, 2) + jnp.roll(values, -2, 2))
    return (along_y + along_x - 60.0 * values) / 12.0


def slope(values, plane):
    total = diffraction * laplace(values) + phase_gain * plane.astype(jnp.float32) * values
    return jnp.stack([-total[1], total[0]])


def reference(optical_field, index_panels):
    field = optical_field
    for step_index in range(STEPS):
        first = 2 * step_index
        first_slope = slope(field, index_panels[first])
        second_slope = slope(field + 0.5 * first_slope, index_panels[first + 1])
        third_slope = slope(field + 0.5 * second_slope, index_panels[first + 1])
        fourth_slope = slope(field + third_slope, index_panels[first + 2])
        field = field + (first_slope + 2.0 * second_slope + 2.0 * third_slope + fourth_slope) / 6.0
    return field
```

```python
import functools

import jax
import jax.numpy as jnp
from jax import lax
from jax.experimental import pallas as pl
from jax.experimental.pallas import tpu as pltpu
from jax.sharding import PartitionSpec as P

STEPS = 2
MESH = pl.DeviceIdType.MESH
HALO = 16
PAD = 8
LANES = 128

diffraction = 0.15
phase_gain = 0.25
near_gain = diffraction * 16.0 / 12.0
far_gain = diffraction / 12.0
mid = diffraction * 60.0 / 12.0


def kernel(nr, nc, field, panels_in, out, panels, pack, gathered, planes, edges, e, s1, s2, s3,
           strips, side, load_sem, send_sem, plane_recv, edge_send, edge_recv, fwd_send, fwd_recv,
           halo_send, halo_recv, ready_col, ready_row):
    n_planes, part, width = panels.shape
    _, rows, cols = out.shape
    wide = cols + LANES
    sub = HALO // part
    blocks = rows // part
    top = PAD + HALO
    last = n_planes - 1
    pair = 2 * HALO
    half = nc // 2
    r, c = lax.axis_index("row"), lax.axis_index("col")
    up, down = lax.rem(r + nr - 1, nr), lax.rem(r + 1, nr)
    left, right = lax.rem(c + nc - 1, nc), lax.rem(c + 1, nc)
    first_row, last_row = r == 0, r == nr - 1

    barrier = pltpu.get_barrier_semaphore()

    def greet(sem, to):
        pl.semaphore_signal(sem, inc=1, device_id=to, device_id_type=MESH)

    lax.fori_loop(c + 1, nc, lambda k, x: (greet(barrier, (r, k)), x)[1], 0)
    pl.when(jnp.logical_not(last_row))(lambda: greet(barrier, (down, c)))
    pl.when(first_row)(lambda: greet(barrier, (up, c)))

    load_panels = pltpu.make_async_copy(panels_in, panels, load_sem.at[1])
    load_panels.start()
    load_field = pltpu.make_async_copy(field, e.at[:, pl.ds(top, rows), pl.ds(0, cols)], load_sem.at[0])
    load_field.start()
    own_columns = pl.ds(pl.multiple_of(c * cols, LANES), cols)
    own_planes = pltpu.make_async_copy(panels_in.at[:, :, own_columns], planes.at[:, sub + c], load_sem.at[2])
    own_planes.start()

    earlier = c + (r > 0).astype(jnp.int32) + last_row.astype(jnp.int32)
    pl.when(earlier > 0)(lambda: pl.semaphore_wait(barrier, earlier))
    lax.fori_loop(0, c, lambda k, x: (greet(ready_col.at[c], (r, k)), x)[1], 0)
    pl.when(jnp.logical_not(first_row))(lambda: greet(ready_row.at[1], (up, c)))
    pl.when(last_row)(lambda: greet(ready_row.at[0], (down, c)))

    def target(j):
        return lax.rem(j + jnp.where(c < half, half, 0), nc)

    def plane_copy(p, to, at):
        return pltpu.make_async_remote_copy(
            src_ref=panels_in.at[p, :, pl.ds(pl.multiple_of(to * cols, LANES), cols)],
            dst_ref=planes.at[p, sub + at],
            send_sem=send_sem.at[p, to], recv_sem=plane_recv.at[p, at],
            device_id=(r, to), device_id_type=MESH,
        )

    def edge_copy(to, at):
        return pltpu.make_async_remote_copy(
            src_ref=pack.at[to], dst_ref=gathered.at[sub + at],
            send_sem=edge_send.at[to], recv_sem=edge_recv.at[at],
            device_id=(r, to), device_id_type=MESH,
        )

    def others(make, begin=0, end=nc):
        for k in range(begin, end):
            pl.when(k != c)(functools.partial(make, k))

    known = set()

    def meet(j, make):
        to = target(j)

        def go():
            if j not in known:
                pl.when(to > c)(lambda: pl.semaphore_wait(ready_col.at[to], 1))
            make(to).start()

        if j < half:
            go()
        else:
            pl.when(to != c)(go)
        known.add(j)

    def send(p, group):
        for j in group:
            meet(j, lambda to: plane_copy(p, to, c))

    def send_edges(group):
        for j in group:
            meet(j, lambda to: edge_copy(to, c))

    quarter = max(half // 2, 1)
    near, far, local = range(quarter), range(quarter, half), range(half, nc)

    lane = lax.broadcasted_iota(jnp.int32, (part, LANES), 1)
    load_panels.wait()
    for d in range(nc):
        after = (d + 1) * cols % width
        before = (d * cols - LANES) % width
        tile = jnp.zeros((part, LANES), jnp.float32)
        for p in range(last):
            at = pair * p
            tile = jnp.where((lane >= at) & (lane < at + HALO), pltpu.roll(
                panels[p, :, after:after + LANES].astype(jnp.float32), at, 1), tile)
            at += HALO
            tile = jnp.where((lane >= at) & (lane < at + HALO), pltpu.roll(
                panels[p, :, before:before + LANES].astype(jnp.float32), (at + HALO) % LANES, 1), tile)
        pack[d] = tile.astype(pack.dtype)
    send_edges(range(nc))
    gathered[sub + c] = pack[c]

    def remote(src, dst, at, to):
        return pltpu.make_async_remote_copy(
            src_ref=src, dst_ref=dst, send_sem=halo_send.at[at], recv_sem=halo_recv.at[at],
            device_id=to, device_id_type=MESH,
        )

    columns = [
        remote(strips.at[0], side.at[:, pl.ds(0, HALO), :], 0, (r, left)),
        remote(strips.at[1], side.at[:, pl.ds(LANES - HALO, HALO), :], 1, (r, right)),
    ]
    low, high = pl.ds(top, HALO), pl.ds(top + rows - HALO, HALO)
    borders = [
        remote(e.at[:, high, :], e.at[:, pl.ds(PAD, HALO), :], 2, (down, c)),
        remote(e.at[:, low, :], e.at[:, pl.ds(top + rows, HALO), :], 3, (up, c)),
    ]
    load_field.wait()
    for i in range(2):
        strips[0, i] = e[i, top:top + rows, 0:LANES].T[0:HALO]
        strips[1, i] = e[i, top:top + rows, cols - LANES:cols].T[LANES - HALO:LANES]
    for copy in columns:
        copy.start()

    for p in range(n_planes):
        for group in (near, far, local):
            send(p, group)

    for copy in columns:
        copy.wait()
    for i in range(2):
        e[i, top:top + rows, cols:wide] = side[i].T
    pl.when(jnp.logical_not(last_row))(lambda: pl.semaphore_wait(ready_row.at[1], 1))
    pl.when(first_row)(lambda: pl.semaphore_wait(ready_row.at[0], 1))
    for copy in borders:
        copy.start()

    def forwards(ref, at):
        make = lambda src, dst, which, to: pltpu.make_async_remote_copy(
            src_ref=ref.at[pl.ds(src, sub)], dst_ref=ref.at[pl.ds(dst, sub)],
            send_sem=fwd_send.at[at, which], recv_sem=fwd_recv.at[at, which],
            device_id=(to, c), device_id_type=MESH,
        )
        return [make(blocks, 0, 0, down), make(sub, sub + blocks, 1, up)]

    def unpack(begin, end):
        for b in range(begin, end):
            tile = gathered[b].astype(jnp.float32)
            for p in range(last):
                edges[p, b] = jnp.where(
                    lane < LANES // 2,
                    pltpu.roll(tile, (LANES - pair * p) % LANES, 1),
                    pltpu.roll(tile, (LANES - pair * (p + 1)) % LANES, 1),
                ).astype(edges.dtype)

    others(lambda k: edge_copy(k, k).wait_recv())
    edge_forwards = forwards(gathered, last)
    for copy in edge_forwards:
        copy.start()
    unpack(sub, sub + blocks)
    for copy in borders:
        copy.wait()
    own_planes.wait()

    halo_planes = [forwards(planes.at[p], p) for p in range(last)]

    def take(p, begin, end):
        others(lambda k: plane_copy(p, k, k).wait_recv(), begin, end)

    def take_ends(p):
        lower, upper = halo_planes[p]
        take(p, 0, sub)
        upper.start()
        take(p, nc - sub, nc)
        lower.start()

    def take_middle(p):
        take(p, sub, nc - sub)

    def take_halo(p):
        for copy in halo_planes[p]:
            copy.wait()

    def evaluate(src, p, parts, finish):
        for b, shift, count in parts:
            row = b * HALO + shift
            pieces = []
            for i in range(sub):
                piece = planes[p, b * sub + i].astype(jnp.float32)
                edge = edges[min(p, last - 1), b * sub + i].astype(jnp.float32)
                pieces.append(jnp.concatenate([piece, edge], axis=1))
            plane = pieces[0] if sub == 1 else jnp.concatenate(pieces, axis=0)
            factor = phase_gain * plane[shift:shift + count] - mid
            totals = []
            tall = count + 2 * PAD
            for i in range(2):
                window = src[i, row:row + tall, :]
                centre = window[PAD:PAD + count]
                shift_y = lambda n: pltpu.roll(window, n % tall, 0)[PAD:PAD + count]
                shift_x = lambda n: pltpu.roll(centre, n % wide, 1)
                one = (shift_y(1) + shift_y(-1)) + (shift_x(1) + shift_x(-1))
                two = (shift_y(2) + shift_y(-2)) + (shift_x(2) + shift_x(-2))
                totals.append(near_gain * one - far_gain * two + factor * centre)
            finish(slice(row + PAD, row + PAD + count), row - HALO, (-totals[1], totals[0]))

    def stage(dst, weight):
        def finish(at, b, k):
            for i in range(2):
                dst[i, at, :] = e[i, at, :] + weight * k[i]
        return finish

    def close(at, b, k):
        for i in range(2):
            e[i, at, :] = (s1[i, at, :] + 2.0 * s2[i, at, :] + s3[i, at, :] - e[i, at, :]) * (1.0 / 3.0) + k[i] * (1.0 / 6.0)

    def close_out(at, b, k):
        here = slice(b, b + k[0].shape[0])
        for i in range(2):
            value = (s1[i, at, :] + 2.0 * s2[i, at, :] + s3[i, at, :] - e[i, at, :]) * (1.0 / 3.0) + k[i] * (1.0 / 6.0)
            out[i, here, :] = value[:, 0:cols]

    inner = [(b, 0, HALO) for b in range(1, rows // HALO + 1)]
    end = rows // HALO + 1

    def outer(number):
        if HALO - 2 * number > PAD:
            return [(0, 0, HALO), (end, 0, HALO)]
        return [(0, PAD, PAD), (end, 0, PAD)]

    def evaluate_inner(number, src, p, finish):
        evaluate(src, p, inner, finish)

    def evaluate_outer(number, src, p, finish):
        evaluate(src, p, outer(number), finish)

    def evaluate_all(number, src, p, finish):
        first, final = outer(number)
        evaluate(src, p, [first] + inner + [final], finish)

    work = []
    for step in range(STEPS):
        p, number = 2 * step, 4 * step
        work.append((number + 1, e, p, stage(s1, 0.5)))
        work.append((number + 2, s1, p + 1, stage(s2, 0.5)))
        work.append((number + 3, s2, p + 1, stage(s3, 1.0)))
        work.append((number + 4, s3, p + 2, close if step < STEPS - 1 else close_out))

    take_ends(0)
    take_middle(0)
    evaluate_inner(*work[0])
    take_ends(1)
    for copy in edge_forwards:
        copy.wait()
    unpack(0, sub)
    unpack(sub + blocks, 2 * sub + blocks)
    take_halo(0)
    evaluate_outer(*work[0])
    for at in range(1, len(work) - 1):
        p = work[at][2]
        if p == work[at - 1][2]:
            evaluate_all(*work[at])
            continue
        take_middle(p)
        evaluate_inner(*work[at])
        if p + 1 < last:
            take_ends(p + 1)
        take_halo(p)
        evaluate_outer(*work[at])
    take(last, 0, nc)
    evaluate_inner(*work[-1])

    def sent(k):
        edge_copy(k, k).wait_send()
        for p in range(n_planes):
            plane_copy(p, k, k).wait_send()

    others(sent)


def solution(mesh):
    nr, nc = mesh.shape["row"], mesh.shape["col"]

    def local(optical_field, index_panels):
        _, rows, cols = optical_field.shape
        n_planes, part, width = index_panels.shape
        wide = cols + LANES
        count = (rows + 2 * HALO) // part
        tall = rows + 2 * HALO + 2 * PAD
        grid = pltpu.VMEM((2, tall, wide), jnp.float32)
        return pl.pallas_call(
            functools.partial(kernel, nr, nc),
            out_shape=pltpu.VMEM(optical_field.shape, jnp.float32),
            in_specs=[pl.BlockSpec(memory_space=pltpu.HBM)] * 2,
            out_specs=pl.BlockSpec(memory_space=pltpu.VMEM),
            scratch_shapes=[
                pltpu.VMEM((n_planes, part, width), jnp.bfloat16),
                pltpu.VMEM((nc, part, LANES), jnp.bfloat16),
                pltpu.VMEM((count, part, LANES), jnp.bfloat16),
                pltpu.VMEM((n_planes, count, part, cols), jnp.bfloat16),
                pltpu.VMEM((n_planes - 1, count, part, LANES), jnp.bfloat16),
                grid, grid, grid, grid,
                pltpu.VMEM((2, 2, HALO, rows), jnp.float32),
                pltpu.VMEM((2, LANES, rows), jnp.float32),
                pltpu.SemaphoreType.DMA((3,)),
                pltpu.SemaphoreType.DMA((n_planes, nc)),
                pltpu.SemaphoreType.DMA((n_planes, nc)),
                pltpu.SemaphoreType.DMA((nc,)),
                pltpu.SemaphoreType.DMA((nc,)),
                pltpu.SemaphoreType.DMA((n_planes, 2)),
                pltpu.SemaphoreType.DMA((n_planes, 2)),
                pltpu.SemaphoreType.DMA((4,)),
                pltpu.SemaphoreType.DMA((4,)),
                pltpu.SemaphoreType.REGULAR((nc,)),
                pltpu.SemaphoreType.REGULAR((2,)),
            ],
            compiler_params=pltpu.CompilerParams(
                collective_id=0, has_side_effects=True, vmem_limit_bytes=62 * 1024 * 1024),
        )(optical_field, index_panels)

    return jax.shard_map(
        local, mesh=mesh,
        in_specs=(P(None, "row", "col"), P(None, ("row", "col"), None)),
        out_specs=P(None, "row", "col"), check_vma=False,
    )
```

```python
import functools

import jax
import jax.numpy as jnp
from jax import lax
from jax.experimental import pallas as pl
from jax.experimental.pallas import tpu as pltpu
from jax.sharding import PartitionSpec as P

STEPS = 2
MESH = pl.DeviceIdType.MESH
HALO = 16
PAD = 8
LANES = 128

diffraction = 0.15
phase_gain = 0.25
near_gain = diffraction * 16.0 / 12.0
far_gain = diffraction / 12.0
mid = diffraction * 60.0 / 12.0


def kernel(nr, nc, field, panels_in, out, panels, pack, gathered, planes, edges, e, s1, s2, s3,
           strips, side, load_sem, send_sem, plane_recv, fwd_send, fwd_recv,
           halo_send, halo_recv, ready_col, ready_row):
    n_planes, part, width = panels.shape
    _, rows, cols = out.shape
    wide = cols + LANES
    sub = HALO // part
    blocks = rows // part
    top = PAD + HALO
    last = n_planes - 1
    pair = 2 * HALO
    half = nc // 2
    r, c = lax.axis_index("row"), lax.axis_index("col")
    up, down = lax.rem(r + nr - 1, nr), lax.rem(r + 1, nr)
    left, right = lax.rem(c + nc - 1, nc), lax.rem(c + 1, nc)
    first_row, last_row = r == 0, r == nr - 1

    barrier = pltpu.get_barrier_semaphore()

    def greet(sem, to):
        pl.semaphore_signal(sem, inc=1, device_id=to, device_id_type=MESH)

    lax.fori_loop(c + 1, nc, lambda k, x: (greet(barrier, (r, k)), x)[1], 0)
    pl.when(jnp.logical_not(last_row))(lambda: greet(barrier, (down, c)))
    pl.when(first_row)(lambda: greet(barrier, (up, c)))

    load_panels = pltpu.make_async_copy(panels_in, panels, load_sem.at[1])
    load_panels.start()
    load_field = pltpu.make_async_copy(field, e.at[:, pl.ds(top, rows), pl.ds(0, cols)], load_sem.at[0])
    load_field.start()
    own_columns = pl.ds(pl.multiple_of(c * cols, LANES), cols)
    own_planes = pltpu.make_async_copy(
        panels_in.at[pl.ds(1, last), :, own_columns], planes.at[:, sub + c], load_sem.at[2])
    own_planes.start()

    earlier = c + (r > 0).astype(jnp.int32) + last_row.astype(jnp.int32)
    pl.when(earlier > 0)(lambda: pl.semaphore_wait(barrier, earlier))
    lax.fori_loop(0, c, lambda k, x: (greet(ready_col.at[c], (r, k)), x)[1], 0)
    pl.when(jnp.logical_not(first_row))(lambda: greet(ready_row.at[1], (up, c)))
    pl.when(last_row)(lambda: greet(ready_row.at[0], (down, c)))

    def target(j):
        return lax.rem(j + jnp.where(c < half, half, 0), nc)

    def plane_copy(p, to, at):
        columns = pl.ds(pl.multiple_of(to * cols, LANES), cols)
        return pltpu.make_async_remote_copy(
            src_ref=panels.at[p, :, columns] if p > 0 else pack.at[to],
            dst_ref=planes.at[p - 1, sub + at] if p > 0 else gathered.at[sub + at],
            send_sem=send_sem.at[p, to], recv_sem=plane_recv.at[p, at],
            device_id=(r, to), device_id_type=MESH,
        )

    def others(make, begin=0, end=nc):
        for k in range(begin, end):
            pl.when(k != c)(functools.partial(make, k))

    known = set()

    def meet(j, make):
        to = target(j)

        def go():
            if j not in known:
                pl.when((to > c) & (to != right))(lambda: pl.semaphore_wait(ready_col.at[to], 1))
            make(to).start()

        if j < half:
            go()
        else:
            pl.when(to != c)(go)
        known.add(j)

    def send(p, group):
        for j in group:
            meet(j, lambda to: plane_copy(p, to, c))

    quarter = max(half // 2, 1)
    near, far, local = range(quarter), range(quarter, half), range(half, nc)

    lane = lax.broadcasted_iota(jnp.int32, (part, LANES), 1)
    load_panels.wait()
    for d in range(nc):
        after = (d + 1) * cols % width
        before = (d * cols - LANES) % width
        tile = jnp.zeros((part, LANES), jnp.float32)
        for p in range(last):
            at = pair * p
            tile = jnp.where((lane >= at) & (lane < at + HALO), pltpu.roll(
                panels[p, :, after:after + LANES].astype(jnp.float32), at, 1), tile)
            at += HALO
            tile = jnp.where((lane >= at) & (lane < at + HALO), pltpu.roll(
                panels[p, :, before:before + LANES].astype(jnp.float32), (at + HALO) % LANES, 1), tile)
        pack[d, :, 0:cols] = panels[0, :, d * cols:(d + 1) * cols]
        pack[d, :, cols:wide] = tile.astype(pack.dtype)
    gathered[sub + c] = pack[c]

    def remote(src, dst, at, to):
        return pltpu.make_async_remote_copy(
            src_ref=src, dst_ref=dst, send_sem=halo_send.at[at], recv_sem=halo_recv.at[at],
            device_id=to, device_id_type=MESH,
        )

    columns = [
        remote(strips.at[0], side.at[:, pl.ds(0, HALO), :], 0, (r, left)),
        remote(strips.at[1], side.at[:, pl.ds(LANES - HALO, HALO), :], 1, (r, right)),
    ]
    low, high = pl.ds(top, HALO), pl.ds(top + rows - HALO, HALO)
    borders = [
        remote(e.at[:, high, :], e.at[:, pl.ds(PAD, HALO), :], 2, (down, c)),
        remote(e.at[:, low, :], e.at[:, pl.ds(top + rows, HALO), :], 3, (up, c)),
    ]
    load_field.wait()
    for i in range(2):
        strips[0, i] = e[i, top:top + rows, 0:LANES].T[0:HALO]
        strips[1, i] = e[i, top:top + rows, cols - LANES:cols].T[LANES - HALO:LANES]
    pl.when(right > c)(lambda: pl.semaphore_wait(ready_col.at[right], 1))
    columns[1].start()
    pl.when(c > 0)(columns[0].start)

    send(0, near)
    send(0, far)
    send(0, local)
    pl.when(c == 0)(columns[0].start)
    send(1, near)
    send(1, far)
    send(1, local)
    send(2, near)
    send(2, far)
    send(2, local)
    send(3, near)
    send(4, near)
    send(3, local)
    send(4, local)
    send(3, far)
    send(4, far)

    for copy in columns:
        copy.wait()
    for i in range(2):
        e[i, top:top + rows, cols:wide] = side[i].T
    pl.when(jnp.logical_not(last_row))(lambda: pl.semaphore_wait(ready_row.at[1], 1))
    pl.when(first_row)(lambda: pl.semaphore_wait(ready_row.at[0], 1))
    for copy in borders:
        copy.start()

    def forwards(ref, at):
        make = lambda src, dst, which, to: pltpu.make_async_remote_copy(
            src_ref=ref.at[pl.ds(src, sub)], dst_ref=ref.at[pl.ds(dst, sub)],
            send_sem=fwd_send.at[at, which], recv_sem=fwd_recv.at[at, which],
            device_id=(to, c), device_id_type=MESH,
        )
        return [make(blocks, 0, 0, down), make(sub, sub + blocks, 1, up)]

    def unpack(begin, end):
        for b in range(begin, end):
            tile = gathered[b, :, cols:wide].astype(jnp.float32)
            for p in range(last):
                edges[p, b] = jnp.where(
                    lane < LANES // 2,
                    pltpu.roll(tile, (LANES - pair * p) % LANES, 1),
                    pltpu.roll(tile, (LANES - pair * (p + 1)) % LANES, 1),
                ).astype(edges.dtype)

    for copy in borders:
        copy.wait()
    own_planes.wait()

    halo_planes = [forwards(planes.at[p - 1] if p > 0 else gathered, p) for p in range(last)]

    def take(p, begin, end):
        others(lambda k: plane_copy(p, k, k).wait_recv(), begin, end)

    def take_ends(p):
        lower, upper = halo_planes[p]

        def take_first():
            take(p, 0, sub)
            upper.start()

        def take_final():
            take(p, nc - sub, nc)
            lower.start()

        @pl.when(c < half)
        def _():
            take_first()
            take_final()

        @pl.when(c >= half)
        def _():
            take_final()
            take_first()

    def take_middle(p):
        take(p, sub, nc - sub)

    def take_halo(p):
        for copy in halo_planes[p]:
            copy.wait()

    def evaluate(src, p, parts, finish):
        for b, shift, count in parts:
            row = b * HALO + shift
            pieces = []
            for i in range(sub):
                at = b * sub + i
                piece = (planes[p - 1, at] if p > 0 else gathered[at, :, 0:cols]).astype(jnp.float32)
                edge = edges[min(p, last - 1), at].astype(jnp.float32)
                pieces.append(jnp.concatenate([piece, edge], axis=1))
            plane = pieces[0] if sub == 1 else jnp.concatenate(pieces, axis=0)
            factor = phase_gain * plane[shift:shift + count] - mid
            totals = []
            tall = count + 2 * PAD
            for i in range(2):
                window = src[i, row:row + tall, :]
                centre = window[PAD:PAD + count]
                shift_y = lambda n: pltpu.roll(window, n % tall, 0)[PAD:PAD + count]
                shift_x = lambda n: pltpu.roll(centre, n % wide, 1)
                one = (shift_y(1) + shift_y(-1)) + (shift_x(1) + shift_x(-1))
                two = (shift_y(2) + shift_y(-2)) + (shift_x(2) + shift_x(-2))
                totals.append(near_gain * one - far_gain * two + factor * centre)
            finish(slice(row + PAD, row + PAD + count), row - HALO, (-totals[1], totals[0]))

    def stage(dst, weight):
        def finish(at, b, k):
            for i in range(2):
                dst[i, at, :] = e[i, at, :] + weight * k[i]
        return finish

    def close(at, b, k):
        for i in range(2):
            e[i, at, :] = (s1[i, at, :] + 2.0 * s2[i, at, :] + s3[i, at, :] - e[i, at, :]) * (1.0 / 3.0) + k[i] * (1.0 / 6.0)

    def close_out(at, b, k):
        here = slice(b, b + k[0].shape[0])
        for i in range(2):
            value = (s1[i, at, :] + 2.0 * s2[i, at, :] + s3[i, at, :] - e[i, at, :]) * (1.0 / 3.0) + k[i] * (1.0 / 6.0)
            out[i, here, :] = value[:, 0:cols]

    inner = [(b, 0, HALO) for b in range(1, rows // HALO + 1)]
    end = rows // HALO + 1

    def outer(number):
        if HALO - 2 * number > PAD:
            return [(0, 0, HALO), (end, 0, HALO)]
        return [(0, PAD, PAD), (end, 0, PAD)]

    def evaluate_inner(number, src, p, finish):
        evaluate(src, p, inner, finish)

    def evaluate_outer(number, src, p, finish):
        evaluate(src, p, outer(number), finish)

    def evaluate_middle(number, src, p, finish):
        evaluate(src, p, inner[1:-1], finish)

    def evaluate_rest(number, src, p, finish):
        first, final = outer(number)
        evaluate(src, p, [first, inner[0], inner[-1], final], finish)

    work = []
    for step in range(STEPS):
        p, number = 2 * step, 4 * step
        work.append((number + 1, e, p, stage(s1, 0.5)))
        work.append((number + 2, s1, p + 1, stage(s2, 0.5)))
        work.append((number + 3, s2, p + 1, stage(s3, 1.0)))
        work.append((number + 4, s3, p + 2, close if step < STEPS - 1 else close_out))

    take_ends(0)
    take_middle(0)
    unpack(sub, sub + blocks)
    evaluate_inner(*work[0])
    take_ends(1)
    take_halo(0)
    unpack(0, sub)
    unpack(sub + blocks, 2 * sub + blocks)
    evaluate_outer(*work[0])
    for at in range(1, len(work) - 1, 2):
        p = work[at][2]
        take_middle(p)
        evaluate_inner(*work[at])
        if p + 1 < last:
            take_ends(p + 1)
        evaluate_middle(*work[at + 1])
        take_halo(p)
        evaluate_outer(*work[at])
        evaluate_rest(*work[at + 1])
    take(last, 0, nc)
    evaluate_inner(*work[-1])

    def sent(k):
        for p in range(n_planes):
            plane_copy(p, k, k).wait_send()

    others(sent)


def solution(mesh):
    nr, nc = mesh.shape["row"], mesh.shape["col"]

    def local(optical_field, index_panels):
        _, rows, cols = optical_field.shape
        n_planes, part, width = index_panels.shape
        wide = cols + LANES
        count = (rows + 2 * HALO) // part
        tall = rows + 2 * HALO + 2 * PAD
        grid = pltpu.VMEM((2, tall, wide), jnp.float32)
        return pl.pallas_call(
            functools.partial(kernel, nr, nc),
            out_shape=pltpu.VMEM(optical_field.shape, jnp.float32),
            in_specs=[pl.BlockSpec(memory_space=pltpu.HBM)] * 2,
            out_specs=pl.BlockSpec(memory_space=pltpu.VMEM),
            scratch_shapes=[
                pltpu.VMEM((n_planes, part, width), jnp.bfloat16),
                pltpu.VMEM((nc, part, wide), jnp.bfloat16),
                pltpu.VMEM((count, part, wide), jnp.bfloat16),
                pltpu.VMEM((n_planes - 1, count, part, cols), jnp.bfloat16),
                pltpu.VMEM((n_planes - 1, count, part, LANES), jnp.bfloat16),
                grid, grid, grid, grid,
                pltpu.VMEM((2, 2, HALO, rows), jnp.float32),
                pltpu.VMEM((2, LANES, rows), jnp.float32),
                pltpu.SemaphoreType.DMA((3,)),
                pltpu.SemaphoreType.DMA((n_planes, nc)),
                pltpu.SemaphoreType.DMA((n_planes, nc)),
                pltpu.SemaphoreType.DMA((n_planes - 1, 2)),
                pltpu.SemaphoreType.DMA((n_planes - 1, 2)),
                pltpu.SemaphoreType.DMA((4,)),
                pltpu.SemaphoreType.DMA((4,)),
                pltpu.SemaphoreType.REGULAR((nc,)),
                pltpu.SemaphoreType.REGULAR((2,)),
            ],
            compiler_params=pltpu.CompilerParams(
                collective_id=0, has_side_effects=True, vmem_limit_bytes=62 * 1024 * 1024),
        )(optical_field, index_panels)

    return jax.shard_map(
        local, mesh=mesh,
        in_specs=(P(None, "row", "col"), P(None, ("row", "col"), None)),
        out_specs=P(None, "row", "col"), check_vma=False,
    )
```

```python
import functools

import jax
import jax.numpy as jnp
from jax import lax
from jax.experimental import pallas as pl
from jax.experimental.pallas import tpu as pltpu
from jax.sharding import PartitionSpec as P

STEPS = 2
MESH = pl.DeviceIdType.MESH
HALO = 16
PAD = 8
LANES = 128

diffraction = 0.15
phase_gain = 0.25
near_gain = diffraction * 16.0 / 12.0
far_gain = diffraction / 12.0
mid = diffraction * 60.0 / 12.0


def kernel(nr, nc, field, panels_in, out, panels, pack, gathered, planes, edges, e, s1, s2, s3,
           strips, side, load_sem, send_sem, plane_recv, fwd_send, fwd_recv,
           halo_send, halo_recv, ready_col, ready_row):
    n_planes, part, width = panels.shape
    _, rows, cols = out.shape
    wide = cols + LANES
    sub = HALO // part
    blocks = rows // part
    top = PAD + HALO
    last = n_planes - 1
    pair = 2 * HALO
    half = nc // 2
    r, c = lax.axis_index("row"), lax.axis_index("col")
    up, down = lax.rem(r + nr - 1, nr), lax.rem(r + 1, nr)
    left, right = lax.rem(c + nc - 1, nc), lax.rem(c + 1, nc)
    first_row, last_row = r == 0, r == nr - 1

    barrier = pltpu.get_barrier_semaphore()

    def greet(sem, to):
        pl.semaphore_signal(sem, inc=1, device_id=to, device_id_type=MESH)

    lax.fori_loop(c + 1, nc, lambda k, x: (greet(barrier, (r, k)), x)[1], 0)
    pl.when(jnp.logical_not(last_row))(lambda: greet(barrier, (down, c)))
    pl.when(first_row)(lambda: greet(barrier, (up, c)))

    load_panels = pltpu.make_async_copy(panels_in, panels, load_sem.at[1])
    load_panels.start()
    load_field = pltpu.make_async_copy(field, e.at[:, pl.ds(top, rows), pl.ds(0, cols)], load_sem.at[0])
    load_field.start()
    own_columns = pl.ds(pl.multiple_of(c * cols, LANES), cols)
    own_planes = pltpu.make_async_copy(
        panels_in.at[pl.ds(1, last), :, own_columns], planes.at[:, sub + c], load_sem.at[2])
    own_planes.start()

    earlier = c + (r > 0).astype(jnp.int32) + last_row.astype(jnp.int32)
    pl.when(earlier > 0)(lambda: pl.semaphore_wait(barrier, earlier))
    lax.fori_loop(0, c, lambda k, x: (greet(ready_col.at[c], (r, k)), x)[1], 0)
    pl.when(jnp.logical_not(first_row))(lambda: greet(ready_row.at[1], (up, c)))
    pl.when(last_row)(lambda: greet(ready_row.at[0], (down, c)))

    def target(j):
        return lax.rem(j + jnp.where(c < half, half, 0), nc)

    def plane_copy(p, to, at, source=panels):
        columns = pl.ds(pl.multiple_of(to * cols, LANES), cols)
        return pltpu.make_async_remote_copy(
            src_ref=source.at[p, :, columns] if p > 0 else pack.at[to],
            dst_ref=planes.at[p - 1, sub + at] if p > 0 else gathered.at[sub + at],
            send_sem=send_sem.at[p, to], recv_sem=plane_recv.at[p, at],
            device_id=(r, to), device_id_type=MESH,
        )

    def others(make, begin=0, end=nc):
        for k in range(begin, end):
            pl.when(k != c)(functools.partial(make, k))

    known = set()

    def meet(j, make):
        to = target(j)

        def go():
            if j not in known:
                pl.when((to > c) & (to != right) & (to != left))(lambda: pl.semaphore_wait(ready_col.at[to], 1))
            make(to).start()

        if j < half:
            go()
        else:
            pl.when(to != c)(go)
        known.add(j)

    def send(p, group):
        for j in group:
            meet(j, lambda to: plane_copy(p, to, c))

    quarter = max(half // 2, 1)
    near, far, local = range(quarter), range(quarter, half), range(half, nc)

    prompt = c >= half

    @pl.when(prompt)
    def _():
        for j in near:
            plane_copy(1, target(j), c, panels_in).start()

    lane = lax.broadcasted_iota(jnp.int32, (part, LANES), 1)
    load_panels.wait()
    for d in range(nc):
        after = (d + 1) * cols % width
        before = (d * cols - LANES) % width
        tile = jnp.zeros((part, LANES), jnp.float32)
        for p in range(last):
            at = pair * p
            tile = jnp.where((lane >= at) & (lane < at + HALO), pltpu.roll(
                panels[p, :, after:after + LANES].astype(jnp.float32), at, 1), tile)
            at += HALO
            tile = jnp.where((lane >= at) & (lane < at + HALO), pltpu.roll(
                panels[p, :, before:before + LANES].astype(jnp.float32), (at + HALO) % LANES, 1), tile)
        pack[d, :, 0:cols] = panels[0, :, d * cols:(d + 1) * cols]
        pack[d, :, cols:wide] = tile.astype(pack.dtype)
    gathered[sub + c] = pack[c]

    def remote(src, dst, at, to):
        return pltpu.make_async_remote_copy(
            src_ref=src, dst_ref=dst, send_sem=halo_send.at[at], recv_sem=halo_recv.at[at],
            device_id=to, device_id_type=MESH,
        )

    columns = [
        remote(strips.at[0], side.at[:, pl.ds(0, HALO), :], 0, (r, left)),
        remote(strips.at[1], side.at[:, pl.ds(LANES - HALO, HALO), :], 1, (r, right)),
    ]
    low, high = pl.ds(top, HALO), pl.ds(top + rows - HALO, HALO)
    borders = [
        remote(e.at[:, high, :], e.at[:, pl.ds(PAD, HALO), :], 2, (down, c)),
        remote(e.at[:, low, :], e.at[:, pl.ds(top + rows, HALO), :], 3, (up, c)),
    ]
    load_field.wait()
    for i in range(2):
        strips[0, i] = e[i, top:top + rows, 0:LANES].T[0:HALO]
        strips[1, i] = e[i, top:top + rows, cols - LANES:cols].T[LANES - HALO:LANES]
    pl.when(right > c)(lambda: pl.semaphore_wait(ready_col.at[right], 1))
    columns[1].start()
    pl.when(c == 0)(lambda: pl.semaphore_wait(ready_col.at[left], 1))
    columns[0].start()

    send(0, near)
    send(0, far)
    send(0, local)
    pl.when(jnp.logical_not(prompt))(lambda: send(1, near))
    send(1, far)
    send(1, local)
    send(2, near)
    send(2, far)
    send(2, local)
    send(3, near)
    send(4, near)
    send(3, local)
    send(4, local)
    send(3, far)
    send(4, far)

    for copy in columns:
        copy.wait()
    for i in range(2):
        e[i, top:top + rows, cols:wide] = side[i].T
    pl.when(jnp.logical_not(last_row))(lambda: pl.semaphore_wait(ready_row.at[1], 1))
    pl.when(first_row)(lambda: pl.semaphore_wait(ready_row.at[0], 1))
    for copy in borders:
        copy.start()

    def forwards(ref, at):
        make = lambda src, dst, which, to: pltpu.make_async_remote_copy(
            src_ref=ref.at[pl.ds(src, sub)], dst_ref=ref.at[pl.ds(dst, sub)],
            send_sem=fwd_send.at[at, which], recv_sem=fwd_recv.at[at, which],
            device_id=(to, c), device_id_type=MESH,
        )
        return [make(blocks, 0, 0, down), make(sub, sub + blocks, 1, up)]

    def unpack(begin, end):
        for b in range(begin, end):
            tile = gathered[b, :, cols:wide].astype(jnp.float32)
            for p in range(last):
                edges[p, b] = jnp.where(
                    lane < LANES // 2,
                    pltpu.roll(tile, (LANES - pair * p) % LANES, 1),
                    pltpu.roll(tile, (LANES - pair * (p + 1)) % LANES, 1),
                ).astype(edges.dtype)

    for copy in borders:
        copy.wait()
    own_planes.wait()

    halo_planes = [forwards(planes.at[p - 1] if p > 0 else gathered, p) for p in range(last)]

    def take(p, begin, end):
        others(lambda k: plane_copy(p, k, k).wait_recv(), begin, end)

    def take_ends(p):
        lower, upper = halo_planes[p]

        def take_first():
            take(p, 0, sub)
            upper.start()

        def take_final():
            take(p, nc - sub, nc)
            lower.start()

        @pl.when(c < half)
        def _():
            take_first()
            take_final()

        @pl.when(c >= half)
        def _():
            take_final()
            take_first()

    def take_middle(p):
        take(p, sub, nc - sub)

    def take_halo(p):
        for copy in halo_planes[p]:
            copy.wait()

    def evaluate(src, p, parts, finish):
        for b, shift, count in parts:
            row = b * HALO + shift
            pieces = []
            for i in range(sub):
                at = b * sub + i
                piece = (planes[p - 1, at] if p > 0 else gathered[at, :, 0:cols]).astype(jnp.float32)
                edge = edges[min(p, last - 1), at].astype(jnp.float32)
                pieces.append(jnp.concatenate([piece, edge], axis=1))
            plane = pieces[0] if sub == 1 else jnp.concatenate(pieces, axis=0)
            factor = phase_gain * plane[shift:shift + count] - mid
            totals = []
            tall = count + 2 * PAD
            for i in range(2):
                window = src[i, row:row + tall, :]
                centre = window[PAD:PAD + count]
                shift_y = lambda n: pltpu.roll(window, n % tall, 0)[PAD:PAD + count]
                shift_x = lambda n: pltpu.roll(centre, n % wide, 1)
                one = (shift_y(1) + shift_y(-1)) + (shift_x(1) + shift_x(-1))
                short = centre.astype(jnp.bfloat16)
                across = pltpu.roll(short, 2, 1) + pltpu.roll(short, wide - 2, 1)
                two = (shift_y(2) + shift_y(-2)) + across.astype(jnp.float32)
                totals.append(near_gain * one - far_gain * two + factor * centre)
            finish(slice(row + PAD, row + PAD + count), row - HALO, (-totals[1], totals[0]))

    def stage(dst, weight):
        def finish(at, b, k):
            for i in range(2):
                dst[i, at, :] = e[i, at, :] + weight * k[i]
        return finish

    def close(at, b, k):
        for i in range(2):
            e[i, at, :] = (s1[i, at, :] + 2.0 * s2[i, at, :] + s3[i, at, :] - e[i, at, :]) * (1.0 / 3.0) + k[i] * (1.0 / 6.0)

    def close_out(at, b, k):
        here = slice(b, b + k[0].shape[0])
        for i in range(2):
            value = (s1[i, at, :] + 2.0 * s2[i, at, :] + s3[i, at, :] - e[i, at, :]) * (1.0 / 3.0) + k[i] * (1.0 / 6.0)
            out[i, here, :] = value[:, 0:cols]

    inner = [(b, 0, HALO) for b in range(1, rows // HALO + 1)]
    end = rows // HALO + 1

    def outer(number):
        if HALO - 2 * number > PAD:
            return [(0, 0, HALO), (end, 0, HALO)]
        return [(0, PAD, PAD), (end, 0, PAD)]

    def evaluate_inner(number, src, p, finish):
        evaluate(src, p, inner, finish)

    def evaluate_outer(number, src, p, finish):
        evaluate(src, p, outer(number), finish)

    def evaluate_middle(number, src, p, finish):
        evaluate(src, p, inner[1:-1], finish)

    def evaluate_rest(number, src, p, finish):
        first, final = outer(number)
        evaluate(src, p, [first, inner[0], inner[-1], final], finish)

    work = []
    for step in range(STEPS):
        p, number = 2 * step, 4 * step
        work.append((number + 1, e, p, stage(s1, 0.5)))
        work.append((number + 2, s1, p + 1, stage(s2, 0.5)))
        work.append((number + 3, s2, p + 1, stage(s3, 1.0)))
        work.append((number + 4, s3, p + 2, close if step < STEPS - 1 else close_out))

    take_ends(0)
    take_middle(0)
    unpack(sub, sub + blocks)
    evaluate_inner(*work[0])
    take_ends(1)
    take_halo(0)
    unpack(0, sub)
    unpack(sub + blocks, 2 * sub + blocks)
    evaluate_outer(*work[0])
    for at in range(1, len(work) - 1, 2):
        p = work[at][2]
        take_middle(p)
        evaluate_inner(*work[at])
        if p + 1 < last:
            take_ends(p + 1)
        evaluate_middle(*work[at + 1])
        take_halo(p)
        evaluate_outer(*work[at])
        evaluate_rest(*work[at + 1])
    take(last, 0, nc)
    evaluate_inner(*work[-1])

    def sent(k):
        for p in range(n_planes):
            plane_copy(p, k, k).wait_send()

    others(sent)


def solution(mesh):
    nr, nc = mesh.shape["row"], mesh.shape["col"]

    def local(optical_field, index_panels):
        _, rows, cols = optical_field.shape
        n_planes, part, width = index_panels.shape
        wide = cols + LANES
        count = (rows + 2 * HALO) // part
        tall = rows + 2 * HALO + 2 * PAD
        grid = pltpu.VMEM((2, tall, wide), jnp.float32)
        return pl.pallas_call(
            functools.partial(kernel, nr, nc),
            out_shape=pltpu.VMEM(optical_field.shape, jnp.float32),
            in_specs=[pl.BlockSpec(memory_space=pltpu.HBM)] * 2,
            out_specs=pl.BlockSpec(memory_space=pltpu.VMEM),
            scratch_shapes=[
                pltpu.VMEM((n_planes, part, width), jnp.bfloat16),
                pltpu.VMEM((nc, part, wide), jnp.bfloat16),
                pltpu.VMEM((count, part, wide), jnp.bfloat16),
                pltpu.VMEM((n_planes - 1, count, part, cols), jnp.bfloat16),
                pltpu.VMEM((n_planes - 1, count, part, LANES), jnp.bfloat16),
                grid, grid, grid, grid,
                pltpu.VMEM((2, 2, HALO, rows), jnp.float32),
                pltpu.VMEM((2, LANES, rows), jnp.float32),
                pltpu.SemaphoreType.DMA((3,)),
                pltpu.SemaphoreType.DMA((n_planes, nc)),
                pltpu.SemaphoreType.DMA((n_planes, nc)),
                pltpu.SemaphoreType.DMA((n_planes - 1, 2)),
                pltpu.SemaphoreType.DMA((n_planes - 1, 2)),
                pltpu.SemaphoreType.DMA((4,)),
                pltpu.SemaphoreType.DMA((4,)),
                pltpu.SemaphoreType.REGULAR((nc,)),
                pltpu.SemaphoreType.REGULAR((2,)),
            ],
            compiler_params=pltpu.CompilerParams(
                collective_id=0, has_side_effects=True, vmem_limit_bytes=62 * 1024 * 1024),
        )(optical_field, index_panels)

    return jax.shard_map(
        local, mesh=mesh,
        in_specs=(P(None, "row", "col"), P(None, ("row", "col"), None)),
        out_specs=P(None, "row", "col"), check_vma=False,
    )
```

```python
import functools

import jax
import jax.numpy as jnp
from jax import lax
from jax.experimental import pallas as pl
from jax.experimental.pallas import tpu as pltpu
from jax.sharding import PartitionSpec as P

STEPS = 2
MESH = pl.DeviceIdType.MESH
HALO = 16
PAD = 8
LANES = 128

diffraction = 0.15
phase_gain = 0.25
near_gain = diffraction * 16.0 / 12.0
far_gain = diffraction / 12.0
mid = diffraction * 60.0 / 12.0


def kernel(nr, nc, field, panels_in, out, panels, pack, gathered, planes, edges, e, s1, s2, s3,
           strips, side, load_sem, send_sem, plane_recv, fwd_send, fwd_recv,
           halo_send, halo_recv, ready_col, ready_row):
    n_planes, part, width = panels.shape
    _, rows, cols = out.shape
    wide = cols + LANES
    sub = HALO // part
    blocks = rows // part
    top = PAD + HALO
    last = n_planes - 1
    pair = 2 * HALO
    half = nc // 2
    r, c = lax.axis_index("row"), lax.axis_index("col")
    up, down = lax.rem(r + nr - 1, nr), lax.rem(r + 1, nr)
    left, right = lax.rem(c + nc - 1, nc), lax.rem(c + 1, nc)
    first_row, last_row = r == 0, r == nr - 1

    barrier = pltpu.get_barrier_semaphore()

    def greet(sem, to):
        pl.semaphore_signal(sem, inc=1, device_id=to, device_id_type=MESH)

    lax.fori_loop(c + 1, nc, lambda k, x: (greet(barrier, (r, k)), x)[1], 0)
    pl.when(jnp.logical_not(last_row))(lambda: greet(barrier, (down, c)))
    pl.when(first_row)(lambda: greet(barrier, (up, c)))

    load_panels = pltpu.make_async_copy(panels_in, panels, load_sem.at[1])
    load_panels.start()
    load_field = pltpu.make_async_copy(field, e.at[:, pl.ds(top, rows), pl.ds(0, cols)], load_sem.at[0])
    load_field.start()
    own_columns = pl.ds(pl.multiple_of(c * cols, LANES), cols)
    own_planes = pltpu.make_async_copy(
        panels_in.at[pl.ds(1, last), :, own_columns], planes.at[:, sub + c], load_sem.at[2])
    own_planes.start()

    earlier = c + (r > 0).astype(jnp.int32) + last_row.astype(jnp.int32)
    pl.when(earlier > 0)(lambda: pl.semaphore_wait(barrier, earlier))
    lax.fori_loop(0, c, lambda k, x: (greet(ready_col.at[c], (r, k)), x)[1], 0)
    pl.when(jnp.logical_not(first_row))(lambda: greet(ready_row.at[1], (up, c)))
    pl.when(last_row)(lambda: greet(ready_row.at[0], (down, c)))

    def target(j):
        return lax.rem(j + jnp.where(c < half, half, 0), nc)

    def plane_copy(p, to, at, source=panels):
        columns = pl.ds(pl.multiple_of(to * cols, LANES), cols)
        return pltpu.make_async_remote_copy(
            src_ref=source.at[p, :, columns] if p > 0 else pack.at[to],
            dst_ref=planes.at[p - 1, sub + at] if p > 0 else gathered.at[sub + at],
            send_sem=send_sem.at[p, to], recv_sem=plane_recv.at[p, at],
            device_id=(r, to), device_id_type=MESH,
        )

    def others(make, begin=0, end=nc):
        for k in range(begin, end):
            pl.when(k != c)(functools.partial(make, k))

    known = set()

    def meet(j, make):
        to = target(j)

        def go():
            if j not in known:
                pl.when((to > c) & (to != right) & (to != left))(lambda: pl.semaphore_wait(ready_col.at[to], 1))
            make(to).start()

        if j < half:
            go()
        else:
            pl.when(to != c)(go)
        known.add(j)

    def send(p, group):
        for j in group:
            meet(j, lambda to: plane_copy(p, to, c))

    quarter = max(half // 2, 1)
    near, far, local = range(quarter), range(quarter, half), range(half, nc)

    prompt = c >= half

    @pl.when(prompt)
    def _():
        for j in near:
            plane_copy(1, target(j), c, panels_in).start()

    lane = lax.broadcasted_iota(jnp.int32, (part, LANES), 1)
    load_panels.wait()
    for d in range(nc):
        after = (d + 1) * cols % width
        before = (d * cols - LANES) % width
        tile = jnp.zeros((part, LANES), jnp.float32)
        for p in range(last):
            at = pair * p
            tile = jnp.where((lane >= at) & (lane < at + HALO), pltpu.roll(
                panels[p, :, after:after + LANES].astype(jnp.float32), at, 1), tile)
            at += HALO
            tile = jnp.where((lane >= at) & (lane < at + HALO), pltpu.roll(
                panels[p, :, before:before + LANES].astype(jnp.float32), (at + HALO) % LANES, 1), tile)
        pack[d, :, 0:cols] = panels[0, :, d * cols:(d + 1) * cols]
        pack[d, :, cols:wide] = tile.astype(pack.dtype)
    gathered[sub + c] = pack[c]

    def remote(src, dst, at, to):
        return pltpu.make_async_remote_copy(
            src_ref=src, dst_ref=dst, send_sem=halo_send.at[at], recv_sem=halo_recv.at[at],
            device_id=to, device_id_type=MESH,
        )

    columns = [
        remote(strips.at[0], side.at[:, pl.ds(0, HALO), :], 0, (r, left)),
        remote(strips.at[1], side.at[:, pl.ds(LANES - HALO, HALO), :], 1, (r, right)),
    ]
    low, high = pl.ds(top, HALO), pl.ds(top + rows - HALO, HALO)
    borders = [
        remote(e.at[:, high, :], e.at[:, pl.ds(PAD, HALO), :], 2, (down, c)),
        remote(e.at[:, low, :], e.at[:, pl.ds(top + rows, HALO), :], 3, (up, c)),
    ]
    load_field.wait()
    for i in range(2):
        strips[0, i] = e[i, top:top + rows, 0:LANES].T[0:HALO]
        strips[1, i] = e[i, top:top + rows, cols - LANES:cols].T[LANES - HALO:LANES]
    pl.when(right > c)(lambda: pl.semaphore_wait(ready_col.at[right], 1))
    columns[1].start()
    pl.when(c == 0)(lambda: pl.semaphore_wait(ready_col.at[left], 1))
    columns[0].start()

    send(0, near)
    send(0, far)
    send(0, local)
    pl.when(jnp.logical_not(prompt))(lambda: send(1, near))
    send(1, far)
    send(1, local)
    send(2, near)
    send(2, far)
    send(2, local)
    @pl.when(prompt)
    def _():
        send(3, near)
        send(4, near)
        send(3, local)
        send(4, local)
        send(3, far)
        send(4, far)

    @pl.when(jnp.logical_not(prompt))
    def _():
        send(3, near)
        send(3, far)
        send(3, local)
        send(4, near)
        send(4, far)
        send(4, local)


    for copy in columns:
        copy.wait()
    for i in range(2):
        e[i, top:top + rows, cols:wide] = side[i].T
    pl.when(jnp.logical_not(last_row))(lambda: pl.semaphore_wait(ready_row.at[1], 1))
    pl.when(first_row)(lambda: pl.semaphore_wait(ready_row.at[0], 1))
    for copy in borders:
        copy.start()

    def forwards(ref, at):
        make = lambda src, dst, which, to: pltpu.make_async_remote_copy(
            src_ref=ref.at[pl.ds(src, sub)], dst_ref=ref.at[pl.ds(dst, sub)],
            send_sem=fwd_send.at[at, which], recv_sem=fwd_recv.at[at, which],
            device_id=(to, c), device_id_type=MESH,
        )
        return [make(blocks, 0, 0, down), make(sub, sub + blocks, 1, up)]

    def unpack(begin, end):
        for b in range(begin, end):
            tile = gathered[b, :, cols:wide].astype(jnp.float32)
            for p in range(last):
                edges[p, b] = jnp.where(
                    lane < LANES // 2,
                    pltpu.roll(tile, (LANES - pair * p) % LANES, 1),
                    pltpu.roll(tile, (LANES - pair * (p + 1)) % LANES, 1),
                ).astype(edges.dtype)

    for copy in borders:
        copy.wait()
    own_planes.wait()

    halo_planes = [forwards(planes.at[p - 1] if p > 0 else gathered, p) for p in range(last)]

    def take(p, begin, end):
        others(lambda k: plane_copy(p, k, k).wait_recv(), begin, end)

    def take_ends(p):
        lower, upper = halo_planes[p]

        def take_first():
            take(p, 0, sub)
            upper.start()

        def take_final():
            take(p, nc - sub, nc)
            lower.start()

        @pl.when(c < half)
        def _():
            take_first()
            take_final()

        @pl.when(c >= half)
        def _():
            take_final()
            take_first()

    def take_middle(p):
        take(p, sub, nc - sub)

    def take_halo(p):
        for copy in halo_planes[p]:
            copy.wait()

    def evaluate(src, p, parts, finish):
        for b, shift, count in parts:
            row = b * HALO + shift
            pieces = []
            for i in range(sub):
                at = b * sub + i
                piece = (planes[p - 1, at] if p > 0 else gathered[at, :, 0:cols]).astype(jnp.float32)
                edge = edges[min(p, last - 1), at].astype(jnp.float32)
                pieces.append(jnp.concatenate([piece, edge], axis=1))
            plane = pieces[0] if sub == 1 else jnp.concatenate(pieces, axis=0)
            factor = phase_gain * plane[shift:shift + count] - mid
            totals = []
            tall = count + 2 * PAD
            for i in range(2):
                window = src[i, row:row + tall, :]
                centre = window[PAD:PAD + count]
                shift_y = lambda n: pltpu.roll(window, n % tall, 0)[PAD:PAD + count]
                shift_x = lambda n: pltpu.roll(centre, n % wide, 1)
                one = (shift_y(1) + shift_y(-1)) + (shift_x(1) + shift_x(-1))
                short = centre.astype(jnp.bfloat16)
                across = pltpu.roll(short, 2, 1) + pltpu.roll(short, wide - 2, 1)
                two = (shift_y(2) + shift_y(-2)) + across.astype(jnp.float32)
                totals.append(near_gain * one - far_gain * two + factor * centre)
            finish(slice(row + PAD, row + PAD + count), row - HALO, (-totals[1], totals[0]))

    def stage(dst, weight):
        def finish(at, b, k):
            for i in range(2):
                dst[i, at, :] = e[i, at, :] + weight * k[i]
        return finish

    def close(at, b, k):
        for i in range(2):
            e[i, at, :] = (s1[i, at, :] + 2.0 * s2[i, at, :] + s3[i, at, :] - e[i, at, :]) * (1.0 / 3.0) + k[i] * (1.0 / 6.0)

    def close_out(at, b, k):
        here = slice(b, b + k[0].shape[0])
        for i in range(2):
            value = (s1[i, at, :] + 2.0 * s2[i, at, :] + s3[i, at, :] - e[i, at, :]) * (1.0 / 3.0) + k[i] * (1.0 / 6.0)
            out[i, here, :] = value[:, 0:cols]

    inner = [(b, 0, HALO) for b in range(1, rows // HALO + 1)]
    end = rows // HALO + 1

    def outer(number):
        if HALO - 2 * number > PAD:
            return [(0, 0, HALO), (end, 0, HALO)]
        return [(0, PAD, PAD), (end, 0, PAD)]

    def evaluate_inner(number, src, p, finish):
        evaluate(src, p, inner, finish)

    def evaluate_outer(number, src, p, finish):
        evaluate(src, p, outer(number), finish)

    def evaluate_middle(number, src, p, finish):
        evaluate(src, p, inner[1:-1], finish)

    def evaluate_rest(number, src, p, finish):
        first, final = outer(number)
        evaluate(src, p, [first, inner[0], inner[-1], final], finish)

    work = []
    for step in range(STEPS):
        p, number = 2 * step, 4 * step
        work.append((number + 1, e, p, stage(s1, 0.5)))
        work.append((number + 2, s1, p + 1, stage(s2, 0.5)))
        work.append((number + 3, s2, p + 1, stage(s3, 1.0)))
        work.append((number + 4, s3, p + 2, close if step < STEPS - 1 else close_out))

    take_ends(0)
    take_middle(0)
    unpack(sub, sub + blocks)
    evaluate_inner(*work[0])
    take_ends(1)
    take_halo(0)
    unpack(0, sub)
    unpack(sub + blocks, 2 * sub + blocks)
    evaluate_outer(*work[0])
    for at in range(1, len(work) - 1, 2):
        p = work[at][2]
        take_middle(p)
        evaluate_inner(*work[at])
        if p + 1 < last:
            take_ends(p + 1)
        evaluate_middle(*work[at + 1])
        if p + 1 == last:
            break
        take_halo(p)
        evaluate_outer(*work[at])
        evaluate_rest(*work[at + 1])
    number, src, p, finish = work[-1]

    @pl.when(lax.rem(r, 2) == 0)
    def _():
        take_halo(last - 1)
        evaluate_outer(*work[-3])
        evaluate_rest(*work[-2])
        take(last, 0, nc)
        evaluate(src, p, inner, finish)

    @pl.when(lax.rem(r, 2) == 1)
    def _():
        take(last, 0, nc)
        evaluate(src, p, inner[2:-2], finish)
        take_halo(last - 1)
        evaluate_outer(*work[-3])
        evaluate_rest(*work[-2])
        evaluate(src, p, inner[:2] + inner[-2:], finish)

    def sent(k):
        for p in range(n_planes):
            plane_copy(p, k, k).wait_send()

    others(sent)


def solution(mesh):
    nr, nc = mesh.shape["row"], mesh.shape["col"]

    def local(optical_field, index_panels):
        _, rows, cols = optical_field.shape
        n_planes, part, width = index_panels.shape
        wide = cols + LANES
        count = (rows + 2 * HALO) // part
        tall = rows + 2 * HALO + 2 * PAD
        grid = pltpu.VMEM((2, tall, wide), jnp.float32)
        return pl.pallas_call(
            functools.partial(kernel, nr, nc),
            out_shape=pltpu.VMEM(optical_field.shape, jnp.float32),
            in_specs=[pl.BlockSpec(memory_space=pltpu.HBM)] * 2,
            out_specs=pl.BlockSpec(memory_space=pltpu.VMEM),
            scratch_shapes=[
                pltpu.VMEM((n_planes, part, width), jnp.bfloat16),
                pltpu.VMEM((nc, part, wide), jnp.bfloat16),
                pltpu.VMEM((count, part, wide), jnp.bfloat16),
                pltpu.VMEM((n_planes - 1, count, part, cols), jnp.bfloat16),
                pltpu.VMEM((n_planes - 1, count, part, LANES), jnp.bfloat16),
                grid, grid, grid, grid,
                pltpu.VMEM((2, 2, HALO, rows), jnp.float32),
                pltpu.VMEM((2, LANES, rows), jnp.float32),
                pltpu.SemaphoreType.DMA((3,)),
                pltpu.SemaphoreType.DMA((n_planes, nc)),
                pltpu.SemaphoreType.DMA((n_planes, nc)),
                pltpu.SemaphoreType.DMA((n_planes - 1, 2)),
                pltpu.SemaphoreType.DMA((n_planes - 1, 2)),
                pltpu.SemaphoreType.DMA((4,)),
                pltpu.SemaphoreType.DMA((4,)),
                pltpu.SemaphoreType.REGULAR((nc,)),
                pltpu.SemaphoreType.REGULAR((2,)),
            ],
            compiler_params=pltpu.CompilerParams(
                collective_id=0, has_side_effects=True, vmem_limit_bytes=62 * 1024 * 1024),
        )(optical_field, index_panels)

    return jax.shard_map(
        local, mesh=mesh,
        in_specs=(P(None, "row", "col"), P(None, ("row", "col"), None)),
        out_specs=P(None, "row", "col"), check_vma=False,
    )
```
